256 devices in a mesh: freq: 32 (over z, x_hi, core), rec: 8 (over y, x_lo).
Axes of the slice: x: 4 (x_hi: 2, x_lo: 2; x = x_hi * 2 + x_lo), y: 4, z: 8, core: 2. Of those that a mesh axis runs over, the one named last changes fastest.
Arguments:
- kernel: bfloat16 [2, 128, 256, 9216], P(None, 'freq', None, 'rec'), may hold values from -0.09375 to 0.09375
- focusing_in: bfloat16 [64, 9216, 1024], P('freq', 'rec'), may hold values from -6 to 6
- onset_src: int32 [64, 256], P('freq'), may hold values from 128 to 895
- onset_rec: int32 [64, 9216], P('freq', 'rec'), may hold values from 128 to 895
Outputs:
- focusing: bfloat16 [64, 9216, 1024], P('freq', 'rec')
- upgoing_field: bfloat16 [64, 256, 1024], P('freq', 'rec')
The draws below stay inside these ranges and needn't reach their ends.
All inputs are finite; a program needn't handle non-finite values.
Results may differ from the reference program's by a relative error of at most 0.018.
Values may be sent and summed in bfloat16 or wider, within the bound.
No kernel may reach another device: no remote copies, remote signals or barrier semaphores. Data moves between devices by JAX's collectives and lax.ppermute only.
A program may use at most 64 MiB of HBM per device.

```python
import jax
import jax.numpy as jnp
from jax import lax

NR = 9216
S = 256
TRACE_SAMPLES = 1024
LOW = 8
ITERS = 2
NF = 128
FOCAL_POINTS = 64


def plant(result, own_key, smallest, high):
    longest = result.shape.index(max(result.shape))
    spots = []
    for shift in (0, 1):
        where = [jax.random.randint(jax.random.fold_in(own_key, axis), (), 0, length) for axis, length in enumerate(result.shape)]
        where[longest] = (where[longest] + shift) % result.shape[longest]
        spots.append(tuple(where))
    return result.at[spots[0]].set(smallest).at[spots[1]].set(high)


def with_spikes(values, rng, source, target, shards_of, factor):
    def block_of(position):
        return (jnp.arange(values.shape[position]) // (values.shape[position] // shards_of)).reshape((-1,) + (1,) * (values.ndim - 1 - position))

    first = jax.random.permutation(rng, shards_of)[block_of(target)]
    other_side = (block_of(target) + shards_of // 2) % shards_of
    return jnp.where((block_of(source) == first) | (block_of(source) == other_side), factor * values, values)


def block_levels(stream_key, dims, shards, low, largest):
    factor_of = 1.0
    for position, shards_of in shards:
        heights = jax.random.uniform(jax.random.fold_in(jax.random.fold_in(stream_key, 6), position), (shards_of,), jnp.float32, low / len(shards), largest / len(shards))
        factor_of = factor_of * jnp.repeat(jnp.exp(heights), dims[position] // shards_of).reshape((-1,) + (1,) * (len(dims) - 1 - position))
    return factor_of


def gaussian(stream_key, shape, width, bound, shards=(), dtype=jnp.bfloat16):
    result = jax.random.normal(stream_key, shape, jnp.float32) * width
    if len(shards) > 0:
        result = block_levels(stream_key, shape, shards, -0.22, 0.18) * result
    return jnp.clip(result, min=-bound, max=bound).astype(dtype)


def bell_draw_with(stream_key, shape, deviation, limit, shards, heavy, kind=jnp.bfloat16):
    values = deviation * jax.random.normal(stream_key, shape, jnp.float32)
    if shards:
        values = values * block_levels(stream_key, shape, shards, -0.22, 0.18)
    return jnp.clip(with_spikes(values, jax.random.fold_in(stream_key, 3), *heavy), -limit, limit).astype(kind)


def setup_inputs(seed: int = 0) -> dict:
    streams_of = jax.random.split(jax.random.key(seed), 5)
    return {
        "kernel": bell_draw_with(streams_of[0], (2, NF, S, NR), NR ** -0.5, 0.09375, ((1, 32), (3, 8)), (3, 2, 8, 2.0)),
        "focusing_in": gaussian(streams_of[1], (FOCAL_POINTS, NR, TRACE_SAMPLES), 1.0, 6.0, ((0, 32), (1, 8))),
        "onset_src": plant(jax.random.randint(streams_of[2], (FOCAL_POINTS, S), TRACE_SAMPLES // 8, 7 * TRACE_SAMPLES // 8), jax.random.fold_in(streams_of[2], 1), TRACE_SAMPLES // 8, (7 * TRACE_SAMPLES // 8) - 1).astype(jnp.int32),
        "onset_rec": plant(jax.random.randint(streams_of[3], (FOCAL_POINTS, NR), TRACE_SAMPLES // 8, 7 * TRACE_SAMPLES // 8), jax.random.fold_in(streams_of[3], 1), TRACE_SAMPLES // 8, (7 * TRACE_SAMPLES // 8) - 1).astype(jnp.int32),
    }


def make_tables(count, samples, lowest):
    freqs = (lax.iota(jnp.int32, count) + lowest)[:, None]
    times = lax.iota(jnp.int32, samples)[None, :]
    phase = ((freqs * times) % samples).astype(jnp.float32) * (2.0 * 3.141592653589793 / samples)
    both = jnp.stack([jnp.cos(phase), -jnp.sin(phase)])
    forward = both.astype(jnp.bfloat16)
    inverse = (forward.astype(jnp.float32) * (2.0 / samples)).astype(jnp.bfloat16)
    return forward, inverse


def reference(kernel, focusing_in, onset_src, onset_rec):
    band = kernel.shape[1]
    samples = focusing_in.shape[2]
    forward, inverse = make_tables(band, samples, LOW)
    fwd_full = forward.astype(jnp.float32)
    inv_full = inverse.astype(jnp.float32)
    times = lax.iota(jnp.int32, samples)
    keep_src = times[None, None, :] < onset_src[:, :, None]
    keep_rec = times[None, None, :] < onset_rec[:, :, None]
    kernel_spectral = jnp.moveaxis(kernel, 1, 0)

    def forward_one(pair):
        block_slice, spec = pair
        b0 = block_slice[0].astype(jnp.float32)
        b1 = block_slice[1].astype(jnp.float32)
        s0 = spec[0].astype(jnp.float32)
        s1 = spec[1].astype(jnp.float32)
        real = jnp.dot(b0, s0.T, preferred_element_type=jnp.float32) - jnp.dot(b1, s1.T, preferred_element_type=jnp.float32)
        imag = jnp.dot(b0, s1.T, preferred_element_type=jnp.float32) + jnp.dot(b1, s0.T, preferred_element_type=jnp.float32)
        return jnp.stack([real, imag])

    def adjoint_one(pair):
        block_slice, spec = pair
        b0 = block_slice[0].astype(jnp.float32)
        b1 = block_slice[1].astype(jnp.float32)
        h0 = spec[0].astype(jnp.float32)
        h1 = spec[1].astype(jnp.float32)
        real = jnp.dot(b0.T, h0, preferred_element_type=jnp.float32) + jnp.dot(b1.T, h1, preferred_element_type=jnp.float32)
        imag = jnp.dot(b0.T, h1, preferred_element_type=jnp.float32) - jnp.dot(b1.T, h0, preferred_element_type=jnp.float32)
        return jnp.stack([real, imag])

    focusing = focusing_in
    upgoing_field = None
    for step in range(ITERS):
        spectrum = jnp.einsum("prt,ckt->kcpr", focusing.astype(jnp.float32), fwd_full).astype(jnp.bfloat16)
        sums = lax.map(forward_one, (kernel_spectral, spectrum)).astype(jnp.bfloat16)
        signal = jnp.einsum("kcsp,ckt->pst", sums.astype(jnp.float32), inv_full)
        upgoing_field = signal.astype(jnp.bfloat16)
        muted = jnp.where(keep_src, signal, jnp.float32(0.0)).astype(jnp.bfloat16)
        echo = jnp.einsum("pst,ckt->kcsp", muted.astype(jnp.float32), fwd_full).astype(jnp.bfloat16)
        reflected = lax.map(adjoint_one, (kernel_spectral, echo)).astype(jnp.bfloat16)
        update = jnp.einsum("kcrp,ckt->prt", reflected.astype(jnp.float32), inv_full)
        focusing = (focusing_in.astype(jnp.float32) + jnp.where(keep_rec, update, jnp.float32(0.0))).astype(jnp.bfloat16)
    return (focusing, upgoing_field)
```

```python
import functools

import jax
import jax.numpy as jnp
import numpy as np
from jax import lax
from jax.experimental import pallas as pl
from jax.experimental.pallas import tpu as pltpu
from jax.sharding import PartitionSpec as P

LOW = 8
ITERS = 2
SPLIT = False
F32 = jnp.float32
BF16 = jnp.bfloat16
NN = (((1,), (0,)), ((), ()))
NT = (((1,), (1,)), ((), ()))
TN = (((0,), (0,)), ((), ()))


def dot(a, b, dims=NN):
    return lax.dot_general(a, b, dims, preferred_element_type=F32)


def make_table(freq, own, samples):
    k = np.arange(freq * own)[:, None] + LOW
    t = np.arange(samples)[None, :]
    phase = ((k * t) % samples).astype(np.float32) * np.float32(2.0 * 3.141592653589793 / samples)
    both = np.stack([np.cos(phase), -np.sin(phase)]).astype(np.float32)
    rows = both.reshape(2, freq, own, samples).transpose(1, 0, 2, 3)
    return jnp.asarray(rows.reshape(freq * 2 * own, samples), BF16)


def make_order(freq, points, own):
    n = freq * points * 2 * own
    rows = np.arange(n).reshape(freq, points, 2, own).transpose(3, 2, 0, 1).reshape(n)
    return jnp.asarray(np.eye(n, dtype=np.float32)[rows], BF16)


def make_pairs(freq, points):
    n = freq * points * 2
    rows = np.arange(n).reshape(2, freq, points).transpose(1, 2, 0).reshape(n)
    return jnp.asarray(np.eye(n, dtype=np.float32)[rows], BF16)


def whole(shape):
    return pl.BlockSpec(shape, lambda *_: (0,) * len(shape))


def cost(flops, bytes_accessed):
    return pl.CostEstimate(flops=int(flops), transcendentals=0, bytes_accessed=int(bytes_accessed))


def spectrum_rows(fs, table, freq):
    parts = [dot(table, f, NT) for f in fs]
    parts = [s.reshape(freq, s.shape[0] // freq, s.shape[1]) for s in parts]
    return jnp.concatenate(parts, axis=1).astype(BF16)


def spectrum_kernel(f_ref, table_ref, out_ref):
    fs = [f_ref[p] for p in range(f_ref.shape[0])]
    out_ref[...] = spectrum_rows(fs, table_ref[...], out_ref.shape[0])


def spectrum(f, table, freq, block=384):
    points, receivers, samples = f.shape
    rows = points * table.shape[0] // freq
    return pl.pallas_call(
        spectrum_kernel,
        grid=(receivers // block,),
        in_specs=[pl.BlockSpec((points, block, samples), lambda i: (0, i, 0)), whole(table.shape)],
        out_specs=pl.BlockSpec((freq, rows, block), lambda i: (0, 0, i)),
        out_shape=jax.ShapeDtypeStruct((freq, rows, receivers), BF16),
        cost_estimate=cost(2 * f.size * table.shape[0], 2 * (f.size + freq * rows * receivers)),
        name="spectrum",
    )(f, table)


def product_kernel(k_ref, x_ref, order_ref, pairs_ref, out_ref, w, g):
    step = pl.program_id(0)
    own, rows, receivers = w.shape
    half = rows // 2
    blocks, _, width = out_ref.shape
    share = width // own

    @pl.when(step == 0)
    def _():
        x = x_ref[...].reshape(own * rows, receivers)
        w[...] = dot(order_ref[...], x).astype(BF16).reshape(w.shape)

    w0 = w[step]
    w1 = jnp.concatenate([-w0[half:], w0[:half]], axis=0)
    total = dot(w0, k_ref[0, 0], NT) + dot(w1, k_ref[1, 0], NT)
    g[step] = dot(pairs_ref[...], total.astype(BF16))

    @pl.when(step == own - 1)
    def _():
        for j in range(blocks):
            parts = [g[kk, :, j * share : (j + 1) * share] for kk in range(own)]
            out_ref[j] = jnp.concatenate(parts, axis=1).astype(BF16)


def product(kernel, x, order, pairs, blocks):
    _, own, sources, receivers = kernel.shape
    rows = order.shape[0] // own
    width = own * sources // blocks
    return pl.pallas_call(
        product_kernel,
        grid=(own,),
        in_specs=[
            pl.BlockSpec((2, 1, sources, receivers), lambda i: (0, i, 0, 0)),
            whole(x.shape),
            whole(order.shape),
            whole(pairs.shape),
        ],
        out_specs=whole((blocks, rows, width)),
        out_shape=jax.ShapeDtypeStruct((blocks, rows, width), BF16),
        scratch_shapes=[
            pltpu.VMEM((own, rows, receivers), BF16),
            pltpu.VMEM((own, rows, sources), F32),
        ],
        cost_estimate=cost(2 * kernel.size * rows, 2 * (kernel.size + x.size)),
        name="product",
    )(kernel, x, order, pairs)


def source_kernel(points, keep_field, v_ref, onset_ref, table_ref, h_ref, *field_ref):
    rows, samples = table_ref.shape
    lines, width = h_ref.shape
    share = onset_ref.shape[1]
    own = width // share
    table = table_ref[...]
    v = v_ref[...].astype(F32)
    if v.ndim == 3:
        v = jnp.sum(v, axis=0)
    v = v.astype(BF16)
    row = lax.broadcasted_iota(jnp.int32, (rows, lines), 0)
    line = lax.broadcasted_iota(jnp.int32, (rows, lines), 1)
    device, part, mine = row // (2 * own), row // own % 2, row % own
    h = [jnp.zeros((lines, share), F32) for _ in range(own)]
    for p in range(points):
        at = (device * points + p) * 2 + part
        picks = [jnp.where((line == at) & (mine == kk), 1.0, 0.0).astype(BF16) for kk in range(own)]
        full = jnp.zeros((rows, share), F32)
        for kk in range(own):
            full = full + dot(picks[kk], v[:, kk * share : (kk + 1) * share])
        g = dot(full.astype(BF16), table, TN) * (2.0 / samples)
        if keep_field:
            field_ref[0][p] = g.astype(BF16)
        times = lax.broadcasted_iota(jnp.int32, g.shape, 1)
        muted = jnp.where(times < onset_ref[p], g, 0.0).astype(BF16)
        back = dot(table, muted, NT).astype(BF16)
        for kk in range(own):
            h[kk] = h[kk] + dot(picks[kk], back, TN)
    h_ref[...] = jnp.concatenate(h, axis=1).astype(BF16)


def source_step(v, onset, table, keep_field):
    samples = table.shape[1]
    points, share, _ = onset.shape
    out_shape = [jax.ShapeDtypeStruct(v.shape[-2:], BF16)]
    if keep_field:
        out_shape.append(jax.ShapeDtypeStruct((points, share, samples), BF16))
    return pl.pallas_call(
        functools.partial(source_kernel, points, keep_field),
        out_shape=out_shape,
        cost_estimate=cost(4 * v.size * samples, 2 * table.size),
        name="source",
    )(v, onset, table)


def adjoint_kernel(k_ref, u_ref, pairs_ref, order_ref, out_ref, l, o):
    step = pl.program_id(0)
    own, rows, _ = l.shape
    half = rows // 2
    blocks, _, width = u_ref.shape
    share = width // own

    @pl.when(step == 0)
    def _():
        for kk in range(own):
            parts = [u_ref[j, :, kk * share : (kk + 1) * share] for j in range(blocks)]
            full = jnp.concatenate(parts, axis=1)
            l[kk] = dot(pairs_ref[...], full, TN).astype(BF16)

    l0 = l[step]
    l1 = jnp.concatenate([l0[half:], -l0[:half]], axis=0)
    o[step] = (dot(l0, k_ref[0, 0]) + dot(l1, k_ref[1, 0])).astype(BF16)

    @pl.when(step == own - 1)
    def _():
        flat = o[...].reshape(own * rows, o.shape[2])
        out_ref[...] = dot(order_ref[...], flat, TN).astype(BF16).reshape(out_ref.shape)


def adjoint(kernel, u, pairs, order, freq):
    _, own, sources, receivers = kernel.shape
    rows = u.shape[1]
    out = (freq, own * rows // freq, receivers)
    return pl.pallas_call(
        adjoint_kernel,
        grid=(own,),
        in_specs=[
            pl.BlockSpec((2, 1, sources, receivers), lambda i: (0, i, 0, 0)),
            whole(u.shape),
            whole(pairs.shape),
            whole(order.shape),
        ],
        out_specs=whole(out),
        out_shape=jax.ShapeDtypeStruct(out, BF16),
        scratch_shapes=[
            pltpu.VMEM((own, rows, sources), BF16),
            pltpu.VMEM((own, rows, receivers), BF16),
        ],
        cost_estimate=cost(2 * kernel.size * rows, 2 * (kernel.size + own * rows * receivers)),
        name="adjoint",
    )(kernel, u, pairs, order)


def update_kernel(last, q_ref, f_ref, onset_ref, table_ref, out_ref):
    table = table_ref[...]
    freq, rows, block = q_ref.shape
    points, _, samples = f_ref.shape
    each = rows // points
    spectra = q_ref[...].astype(F32)
    times = lax.broadcasted_iota(jnp.int32, (block, samples), 1)
    fs = []
    for p in range(points):
        mine = spectra[:, p * each : (p + 1) * each].reshape(freq * each, block).astype(BF16)
        q = dot(mine, table, TN) * (2.0 / samples)
        f = f_ref[p].astype(F32) + jnp.where(times < onset_ref[p], q, 0.0)
        fs.append(f.astype(BF16))
    if last:
        for p in range(points):
            out_ref[p] = fs[p]
    else:
        out_ref[...] = spectrum_rows(fs, table, freq)


def update(q, f, onset, table, last, block=384):
    points, receivers, samples = f.shape
    freq, rows, _ = q.shape
    spec_block = pl.BlockSpec((freq, rows, block), lambda i: (0, 0, i))
    trace_block = pl.BlockSpec((points, block, samples), lambda i: (0, i, 0))
    return pl.pallas_call(
        functools.partial(update_kernel, last),
        grid=(receivers // block,),
        in_specs=[spec_block, trace_block, pl.BlockSpec((points, block, 1), lambda i: (0, i, 0)), whole(table.shape)],
        out_specs=trace_block if last else spec_block,
        out_shape=jax.ShapeDtypeStruct(f.shape if last else q.shape, BF16),
        cost_estimate=cost(4 * f.size * table.shape[0], 2 * (2 * f.size + q.size)),
        name="update",
    )(q, f, onset, table)


def exchange(x, axis):
    return lax.all_to_all(x, axis, split_axis=0, concat_axis=0, tiled=True)


def body(kernel, focusing_in, onset_src, onset_rec):
    freq = lax.axis_size("freq")
    rec = lax.axis_size("rec")
    _, own, sources, receivers = kernel.shape
    points, _, samples = focusing_in.shape
    share = sources // rec
    lines, width = freq * points * 2, own * share
    table = make_table(freq, own, samples)
    order = make_order(freq, points, own)
    pairs = make_pairs(freq, points)
    first = lax.axis_index("rec") * share
    src_onsets = lax.dynamic_slice_in_dim(onset_src, first, share, 1)[:, :, None]
    rec_onsets = onset_rec[:, :, None]
    spec = spectrum(focusing_in, table, freq)
    field = None
    for step in range(ITERS):
        last = step == ITERS - 1
        part = product(kernel, exchange(spec, "freq"), order, pairs, rec)
        if SPLIT:
            v = jnp.sum(exchange(part, "rec").astype(F32), axis=0).astype(BF16)
            v = exchange(v.reshape(freq, points * 2, width), "freq").reshape(lines, width)
        else:
            v = exchange(part.reshape(rec * freq, points * 2, width), ("rec", "freq"))
            v = v.reshape(rec, lines, width)
        h, *kept = source_step(v, src_onsets, table, last)
        if last:
            field = kept[0]
        if SPLIT:
            u = exchange(h.reshape(freq, points * 2, width), "freq").reshape(1, lines, width)
            u = exchange(jnp.broadcast_to(u, (rec, lines, width)), "rec")
        else:
            u = jnp.broadcast_to(h.reshape(1, freq, points * 2, width), (rec, freq, points * 2, width))
            u = exchange(u.reshape(rec * freq, points * 2, width), ("rec", "freq")).reshape(rec, lines, width)
        q = exchange(adjoint(kernel, u, pairs, order, freq), "freq")
        spec = update(q, focusing_in, rec_onsets, table, last)
    return spec, field


def solution(mesh):
    placed = (
        P(None, "freq", None, "rec"),
        P("freq", "rec", None),
        P("freq", None),
        P("freq", "rec"),
    )
    return jax.shard_map(
        body,
        mesh=mesh,
        in_specs=placed,
        out_specs=(P("freq", "rec", None), P("freq", "rec", None)),
        check_vma=False,
    )
```

```python
import functools

import jax
import jax.numpy as jnp
import numpy as np
from jax import lax
from jax.experimental import pallas as pl
from jax.experimental.pallas import tpu as pltpu
from jax.sharding import PartitionSpec as P

LOW = 8
ITERS = 2
F32 = jnp.float32
BF16 = jnp.bfloat16
NN = (((1,), (0,)), ((), ()))
NT = (((1,), (1,)), ((), ()))
TN = (((0,), (0,)), ((), ()))


def dot(a, b, dims=NN):
    return lax.dot_general(a, b, dims, preferred_element_type=F32)


def make_table(freq, own, samples):
    k = np.arange(freq * own)[:, None] + LOW
    t = np.arange(samples)[None, :]
    phase = ((k * t) % samples).astype(np.float32) * np.float32(2.0 * 3.141592653589793 / samples)
    both = np.stack([np.cos(phase), -np.sin(phase)]).astype(np.float32)
    rows = both.reshape(2, freq, own, samples).transpose(1, 0, 2, 3)
    return jnp.asarray(rows.reshape(freq * 2 * own, samples), BF16)


def make_order(freq, points, own):
    n = freq * points * 2 * own
    rows = np.arange(n).reshape(freq, points, 2, own).transpose(3, 2, 0, 1).reshape(n)
    return jnp.asarray(np.eye(n, dtype=np.float32)[rows], BF16)


def make_pairs(freq, points):
    n = freq * points * 2
    rows = np.arange(n).reshape(2, freq, points).transpose(1, 2, 0).reshape(n)
    return jnp.asarray(np.eye(n, dtype=np.float32)[rows], BF16)


VSPEC = pl.BlockSpec(memory_space=pltpu.VMEM)
ANY = pl.BlockSpec(memory_space=pl.ANY)
PARAMS = pltpu.CompilerParams(vmem_limit_bytes=24 << 20)


def vmem(x):
    return pltpu.with_memory_space_constraint(x, pltpu.VMEM)


def hbm(x):
    return pltpu.with_memory_space_constraint(x, pltpu.HBM)


def vout(shape):
    return pltpu.VMEM(shape, BF16)


def cost(flops, bytes_accessed):
    return pl.CostEstimate(flops=int(flops), transcendentals=0, bytes_accessed=int(bytes_accessed))


def pieces(length, size):
    return [slice(at, min(at + size, length)) for at in range(0, length, size)]


def spectrum_kernel(f_hbm, table_hbm, out_ref, f_buf, table_buf, sems):
    freq = out_ref.shape[0]
    points, receivers, _ = f_buf.shape
    ats = pieces(receivers, 256)
    copies = [pltpu.make_async_copy(f_hbm.at[:, at], f_buf.at[:, at], sems.at[i]) for i, at in enumerate(ats)]
    table_copy = pltpu.make_async_copy(table_hbm, table_buf, sems.at[len(ats)])
    table_copy.start()
    copies[0].start()
    table_copy.wait()
    copies[1].start()
    for i, at in enumerate(ats):
        copies[i].wait()
        if i + 2 < len(ats):
            copies[i + 2].start()
        parts = [dot(table_buf[...], f_buf[p, at], NT) for p in range(points)]
        parts = [s.reshape(freq, s.shape[0] // freq, s.shape[1]) for s in parts]
        out_ref[:, :, at] = jnp.concatenate(parts, axis=1).astype(BF16)


def spectrum(f, table, freq):
    points, receivers, _ = f.shape
    rows = points * table.shape[0] // freq
    return pl.pallas_call(
        spectrum_kernel,
        in_specs=[ANY, ANY],
        out_specs=VSPEC,
        out_shape=jax.ShapeDtypeStruct((freq, rows, receivers), BF16),
        scratch_shapes=[
            pltpu.VMEM(f.shape, BF16),
            pltpu.VMEM(table.shape, BF16),
            pltpu.SemaphoreType.DMA((len(pieces(receivers, 256)) + 1,)),
        ],
        compiler_params=PARAMS,
        cost_estimate=cost(2 * f.size * table.shape[0], 2 * (f.size + freq * rows * receivers)),
        name="spectrum",
    )(hbm(f), hbm(table))


def product_kernel(k_hbm, x_ref, order_ref, pairs_ref, late_ref, out_ref, k_buf, w, sems):
    own, rows, receivers = w.shape
    half = rows // 2
    blocks, _, width = out_ref.shape
    share = width // own
    copies = [pltpu.make_async_copy(k_hbm.at[:, kk], k_buf.at[:, kk], sems.at[kk]) for kk in range(own)]
    for copy in copies[:2]:
        copy.start()
    x = x_ref[...].reshape(own * rows, receivers)
    w[...] = dot(order_ref[...], x).astype(BF16).reshape(w.shape)
    g = []
    for kk in range(own):
        w0 = w[kk]
        w1 = jnp.concatenate([-w0[half:], w0[:half]], axis=0)
        copies[kk].wait()
        if kk + 2 < own:
            copies[kk + 2].start()
        total = dot(k_buf[0, kk], w0, NT) + dot(k_buf[1, kk], w1, NT)
        g.append(dot(pairs_ref[...], total.astype(BF16), NT))
    for j in range(blocks):
        parts = [g[kk][:, j * share : (j + 1) * share] for kk in range(own)]
        out_ref[j] = jnp.concatenate(parts, axis=1).astype(BF16)


def product(kernel, x, order, pairs, late, blocks):
    _, own, sources, receivers = kernel.shape
    rows = order.shape[0] // own
    width = own * sources // blocks
    return pl.pallas_call(
        product_kernel,
        in_specs=[ANY, VSPEC, VSPEC, VSPEC, ANY],
        out_specs=[VSPEC, VSPEC],
        out_shape=[vout((blocks, rows, width)), vout(kernel.shape)],
        scratch_shapes=[pltpu.VMEM((own, rows, receivers), BF16), pltpu.SemaphoreType.DMA((own,))],
        compiler_params=PARAMS,
        cost_estimate=cost(2 * kernel.size * rows, 2 * (kernel.size + x.size)),
        name="product",
    )(hbm(kernel), vmem(x), vmem(order), vmem(pairs), late)


def source_kernel(points, keep_field, v_ref, onset_ref, table_ref, h_ref, *field_ref):
    rows, samples = table_ref.shape
    copies, lines, width = h_ref.shape
    share = onset_ref.shape[1]
    own = width // share
    table = table_ref[...]
    v = v_ref[...].astype(F32)
    if v.ndim == 3:
        v = jnp.sum(v, axis=0)
    v = v.astype(BF16)
    row = lax.broadcasted_iota(jnp.int32, (rows, lines), 0)
    line = lax.broadcasted_iota(jnp.int32, (rows, lines), 1)
    device, part, mine = row // (2 * own), row // own % 2, row % own
    h = [jnp.zeros((lines, share), F32) for _ in range(own)]
    for p in range(points):
        at = (device * points + p) * 2 + part
        picks = [jnp.where((line == at) & (mine == kk), 1.0, 0.0).astype(BF16) for kk in range(own)]
        full = jnp.zeros((rows, share), F32)
        for kk in range(own):
            full = full + dot(picks[kk], v[:, kk * share : (kk + 1) * share])
        g = dot(full.astype(BF16), table, TN) * (2.0 / samples)
        if keep_field:
            field_ref[0][p] = g.astype(BF16)
        times = lax.broadcasted_iota(jnp.int32, g.shape, 1)
        muted = jnp.where(times < onset_ref[p], g, 0.0).astype(BF16)
        back = dot(table, muted, NT).astype(BF16)
        for kk in range(own):
            h[kk] = h[kk] + dot(picks[kk], back, TN)
    full = jnp.concatenate(h, axis=1).astype(BF16)
    for j in range(copies):
        h_ref[j] = full


def source_step(v, onset, table, keep_field, copies):
    samples = table.shape[1]
    points, share, _ = onset.shape
    out_shape = [vout((copies,) + v.shape[-2:])]
    if keep_field:
        out_shape.append(jax.ShapeDtypeStruct((points, share, samples), BF16))
    return pl.pallas_call(
        functools.partial(source_kernel, points, keep_field),
        in_specs=[VSPEC] * 3,
        out_specs=[VSPEC] * len(out_shape),
        out_shape=out_shape,
        compiler_params=PARAMS,
        cost_estimate=cost(4 * v.size * samples, 2 * table.size),
        name="source",
    )(vmem(v), vmem(onset), vmem(table))


def adjoint_kernel(k_ref, u_ref, pairs_ref, order_ref, out_ref, o):
    own, rows, receivers = o.shape
    half = rows // 2
    blocks, _, width = u_ref.shape
    share = width // own
    for kk in range(own):
        parts = [u_ref[j, :, kk * share : (kk + 1) * share] for j in range(blocks)]
        l0 = dot(pairs_ref[...], jnp.concatenate(parts, axis=1), TN).astype(BF16)
        l1 = jnp.concatenate([l0[half:], -l0[:half]], axis=0)
        o[kk] = (dot(l0, k_ref[0, kk]) + dot(l1, k_ref[1, kk])).astype(BF16)
    flat = o[...].reshape(own * rows, receivers)
    out_ref[...] = dot(order_ref[...], flat, TN).astype(BF16).reshape(out_ref.shape)


def adjoint(kernel, u, pairs, order, freq):
    _, own, sources, receivers = kernel.shape
    rows = u.shape[1]
    return pl.pallas_call(
        adjoint_kernel,
        in_specs=[VSPEC] * 4,
        out_specs=VSPEC,
        out_shape=jax.ShapeDtypeStruct((freq, own * rows // freq, receivers), BF16),
        scratch_shapes=[pltpu.VMEM((own, rows, receivers), BF16)],
        compiler_params=PARAMS,
        cost_estimate=cost(2 * kernel.size * rows, 2 * own * rows * receivers),
        name="adjoint",
    )(vmem(kernel), vmem(u), vmem(pairs), vmem(order))


def after_kernel(x_ref, late_ref, out_ref):
    out_ref[...] = x_ref[...]


def after(x, late):
    return pl.pallas_call(
        after_kernel,
        in_specs=[VSPEC, ANY],
        out_specs=VSPEC,
        out_shape=jax.ShapeDtypeStruct(x.shape, x.dtype),
        compiler_params=PARAMS,
        cost_estimate=cost(x.size, 8 * x.size),
        name="after",
    )(x, late)


def own_rows(q, points, p, scale):
    freq, rows, block = q.shape
    each = rows // points
    mine = q.astype(F32)[:, p * each : (p + 1) * each] * scale
    return mine.reshape(freq * each, block).astype(BF16)


def respectrum_kernel(block, q_ref, first_hbm, onset_ref, table_ref, across_ref, out_ref, first_ref, sem):
    copy = pltpu.make_async_copy(first_hbm, first_ref, sem)
    copy.start()
    freq, rows, receivers = q_ref.shape
    samples, _ = across_ref.shape
    points = onset_ref.shape[0]
    for i, at in enumerate(pieces(receivers, block)):
        wide = at.stop - at.start
        times = lax.broadcasted_iota(jnp.int32, (samples, wide), 0)
        parts = []
        for p in range(points):
            q = dot(across_ref[...], own_rows(q_ref[:, :, at], points, p, 2.0 / samples))
            muted = jnp.where(times < onset_ref[p, :, at], q, 0.0).astype(BF16)
            parts.append(dot(table_ref[...], muted).reshape(freq, rows // points, wide))
        if i == 0:
            copy.wait()
        out_ref[:, :, at] = (first_ref[:, :, at].astype(F32) + jnp.concatenate(parts, axis=1)).astype(BF16)


def respectrum(q, first, onset, table, across, block=512):
    freq, rows, receivers = q.shape
    return pl.pallas_call(
        functools.partial(respectrum_kernel, block),
        in_specs=[VSPEC, ANY, VSPEC, VSPEC, VSPEC],
        out_specs=VSPEC,
        out_shape=jax.ShapeDtypeStruct(q.shape, BF16),
        scratch_shapes=[pltpu.VMEM(q.shape, BF16), pltpu.SemaphoreType.DMA],
        compiler_params=PARAMS,
        cost_estimate=cost(4 * q.size * table.shape[1], 6 * q.size),
        name="respectrum",
    )(vmem(q), hbm(first), vmem(onset), vmem(table), vmem(across))


def update_kernel(q_ref, f_ref, onset_ref, table_ref, out_ref):
    points, block, samples = f_ref.shape
    at = pl.ds(pl.program_id(0) * block, block)
    times = lax.broadcasted_iota(jnp.int32, (block, samples), 1)
    for p in range(points):
        q = dot(own_rows(q_ref[:, :, at], points, p, 2.0 / samples), table_ref[...], TN)
        out_ref[p] = (f_ref[p].astype(F32) + jnp.where(times < onset_ref[p], q, 0.0)).astype(BF16)


def update(q, f, onset, table, block=384):
    points, receivers, samples = f.shape
    trace_block = pl.BlockSpec((points, block, samples), lambda i: (0, i, 0))
    return pl.pallas_call(
        update_kernel,
        grid=(receivers // block,),
        in_specs=[VSPEC, trace_block, pl.BlockSpec((points, block, 1), lambda i: (0, i, 0)), VSPEC],
        out_specs=trace_block,
        out_shape=jax.ShapeDtypeStruct(f.shape, BF16),
        compiler_params=PARAMS,
        cost_estimate=cost(2 * f.size * table.shape[0], 2 * (2 * f.size + q.size)),
        name="update",
    )(vmem(q), f, onset, vmem(table))


def exchange(x, axis):
    return lax.all_to_all(x, axis, split_axis=0, concat_axis=0, tiled=True)


def body(kernel, focusing_in, onset_src, onset_rec):
    freq = lax.axis_size("freq")
    rec = lax.axis_size("rec")
    _, own, sources, receivers = kernel.shape
    points, _, samples = focusing_in.shape
    share = sources // rec
    lines, width = freq * points * 2, own * share
    table = make_table(freq, own, samples)
    order = make_order(freq, points, own)
    pairs = make_pairs(freq, points)
    start = spec = spectrum(focusing_in, table, freq)
    own_sources = lax.dynamic_slice_in_dim(after(onset_src, start), lax.axis_index("rec") * share, share, 1)
    late = src_onsets = own_sources[:, :, None]
    for step in range(ITERS):
        last = step == ITERS - 1
        part, held = product(kernel, exchange(spec, "freq"), order, pairs, late, rec)
        v = exchange(part.reshape(rec * freq, points * 2, width), ("rec", "freq")).reshape(rec, lines, width)
        h, *field = source_step(v, src_onsets, table, last, rec)
        u = exchange(h.reshape(rec * freq, points * 2, width), ("rec", "freq")).reshape(rec, lines, width)
        q = adjoint(held, u, pairs, order, freq)
        if last:
            return update(exchange(q, "freq"), focusing_in, late, table), field[0]
        row, across = after(onset_rec, q)[:, None, :], lax.optimization_barrier(table).T
        spec = respectrum(exchange(q, "freq"), start, row, table, across)
        late = after(onset_rec, spec)[:, :, None]


def solution(mesh):
    placed = (
        P(None, "freq", None, "rec"),
        P("freq", "rec", None),
        P("freq", None),
        P("freq", "rec"),
    )
    return jax.shard_map(
        body,
        mesh=mesh,
        in_specs=placed,
        out_specs=(P("freq", "rec", None), P("freq", "rec", None)),
        check_vma=False,
    )
```

```python
import functools

import jax
import jax.numpy as jnp
import numpy as np
from jax import lax
from jax.experimental import pallas as pl
from jax.experimental.pallas import tpu as pltpu
from jax.sharding import PartitionSpec as P

LOW = 8
ITERS = 2
F32 = jnp.float32
BF16 = jnp.bfloat16
NN = (((1,), (0,)), ((), ()))
NT = (((1,), (1,)), ((), ()))
TN = (((0,), (0,)), ((), ()))


def dot(a, b, dims=NN):
    return lax.dot_general(a, b, dims, preferred_element_type=F32)


def make_table(freq, own, samples):
    k = np.arange(freq * own)[:, None] + LOW
    t = np.arange(samples)[None, :]
    phase = ((k * t) % samples).astype(np.float32) * np.float32(2.0 * 3.141592653589793 / samples)
    both = np.stack([np.cos(phase), -np.sin(phase)]).astype(np.float32)
    rows = both.reshape(2, freq, own, samples).transpose(1, 0, 2, 3)
    return jnp.asarray(rows.reshape(freq * 2 * own, samples), BF16)


def make_order(freq, points, own):
    n = freq * points * 2 * own
    rows = np.arange(n).reshape(freq, points, 2, own).transpose(3, 2, 0, 1).reshape(n)
    return jnp.asarray(np.eye(n, dtype=np.float32)[rows], BF16)


def make_pairs(freq, points):
    n = freq * points * 2
    rows = np.arange(n).reshape(2, freq, points).transpose(1, 2, 0).reshape(n)
    return jnp.asarray(np.eye(n, dtype=np.float32)[rows], BF16)


VSPEC = pl.BlockSpec(memory_space=pltpu.VMEM)
ANY = pl.BlockSpec(memory_space=pl.ANY)
PARAMS = pltpu.CompilerParams(vmem_limit_bytes=24 << 20)


def vmem(x):
    return pltpu.with_memory_space_constraint(x, pltpu.VMEM)


def hbm(x):
    return pltpu.with_memory_space_constraint(x, pltpu.HBM)


def vout(shape):
    return pltpu.VMEM(shape, BF16)


def cost(flops, bytes_accessed):
    return pl.CostEstimate(flops=int(flops), transcendentals=0, bytes_accessed=int(bytes_accessed))


def pieces(length, size, first=0):
    edges = [0] + list(range(first or size, length, size)) + [length]
    return [slice(a, b) for a, b in zip(edges[:-1], edges[1:])]


def sends(buf, out, sems, ats):
    return [pltpu.make_async_copy(buf.at[:, :, at], out.at[:, :, at], sems.at[i]) for i, at in enumerate(ats)]


def spectrum_kernel(f_hbm, table_hbm, out_hbm, f_buf, table_buf, out_ref, sems, out_sems):
    freq = out_ref.shape[0]
    points, receivers, _ = f_buf.shape
    ats = pieces(receivers, 512, 256)
    outs = sends(out_ref, out_hbm, out_sems, ats)
    copies = [pltpu.make_async_copy(f_hbm.at[:, at], f_buf.at[:, at], sems.at[i]) for i, at in enumerate(ats)]
    table_copy = pltpu.make_async_copy(table_hbm, table_buf, sems.at[len(ats)])
    table_copy.start()
    copies[0].start()
    table_copy.wait()
    copies[1].start()
    for i, at in enumerate(ats):
        copies[i].wait()
        if i + 2 < len(ats):
            copies[i + 2].start()
        parts = [dot(table_buf[...], f_buf[p, at], NT) for p in range(points)]
        parts = [s.reshape(freq, s.shape[0] // freq, s.shape[1]) for s in parts]
        out_ref[:, :, at] = jnp.concatenate(parts, axis=1).astype(BF16)
        outs[i].start()
    for copy in outs:
        copy.wait()


def spectrum(f, table, freq):
    points, receivers, _ = f.shape
    rows = points * table.shape[0] // freq
    return pl.pallas_call(
        spectrum_kernel,
        in_specs=[ANY, ANY],
        out_specs=ANY,
        out_shape=jax.ShapeDtypeStruct((freq, rows, receivers), BF16),
        scratch_shapes=[
            pltpu.VMEM(f.shape, BF16),
            pltpu.VMEM(table.shape, BF16),
            pltpu.VMEM((freq, rows, receivers), BF16),
            pltpu.SemaphoreType.DMA((len(pieces(receivers, 512, 256)) + 1,)),
            pltpu.SemaphoreType.DMA((len(pieces(receivers, 512, 256)),)),
        ],
        compiler_params=PARAMS,
        cost_estimate=cost(2 * f.size * table.shape[0], 2 * (f.size + freq * rows * receivers)),
        name="spectrum",
    )(hbm(f), hbm(table))


def product_kernel(k_hbm, x_ref, order_ref, pairs_ref, late_ref, out_ref, k_buf, w, sems):
    own, rows, receivers = w.shape
    half = rows // 2
    blocks, _, width = out_ref.shape
    share = width // own
    copies = [pltpu.make_async_copy(k_hbm.at[:, kk], k_buf.at[:, kk], sems.at[kk]) for kk in range(own)]
    for copy in copies[:2]:
        copy.start()
    x = x_ref[...].reshape(own * rows, receivers)
    w[...] = dot(order_ref[...], x).astype(BF16).reshape(w.shape)
    g = []
    for kk in range(own):
        w0 = w[kk]
        w1 = jnp.concatenate([-w0[half:], w0[:half]], axis=0)
        copies[kk].wait()
        if kk + 2 < own:
            copies[kk + 2].start()
        total = dot(k_buf[0, kk], w0, NT) + dot(k_buf[1, kk], w1, NT)
        g.append(dot(pairs_ref[...], total.astype(BF16), NT))
    for j in range(blocks):
        parts = [g[kk][:, j * share : (j + 1) * share] for kk in range(own)]
        out_ref[j] = jnp.concatenate(parts, axis=1).astype(BF16)


def product(kernel, x, order, pairs, late, blocks):
    _, own, sources, receivers = kernel.shape
    rows = order.shape[0] // own
    width = own * sources // blocks
    return pl.pallas_call(
        product_kernel,
        in_specs=[ANY, VSPEC, VSPEC, VSPEC, ANY],
        out_specs=[VSPEC, VSPEC],
        out_shape=[vout((blocks, rows, width)), vout(kernel.shape)],
        scratch_shapes=[pltpu.VMEM((own, rows, receivers), BF16), pltpu.SemaphoreType.DMA((own,))],
        compiler_params=PARAMS,
        cost_estimate=cost(2 * kernel.size * rows, 2 * (kernel.size + x.size)),
        name="product",
    )(hbm(kernel), vmem(x), vmem(order), vmem(pairs), late)


def source_kernel(points, keep_field, v_ref, onset_ref, table_ref, h_ref, *field_ref):
    rows, samples = table_ref.shape
    copies, lines, width = h_ref.shape
    share = onset_ref.shape[1]
    own = width // share
    table = table_ref[...]
    v = v_ref[...].astype(F32)
    if v.ndim == 3:
        v = jnp.sum(v, axis=0)
    v = v.astype(BF16)
    row = lax.broadcasted_iota(jnp.int32, (rows, lines), 0)
    line = lax.broadcasted_iota(jnp.int32, (rows, lines), 1)
    device, part, mine = row // (2 * own), row // own % 2, row % own
    h = [jnp.zeros((lines, share), F32) for _ in range(own)]
    for p in range(points):
        at = (device * points + p) * 2 + part
        picks = [jnp.where((line == at) & (mine == kk), 1.0, 0.0).astype(BF16) for kk in range(own)]
        full = jnp.zeros((rows, share), F32)
        for kk in range(own):
            full = full + dot(picks[kk], v[:, kk * share : (kk + 1) * share])
        g = dot(full.astype(BF16), table, TN) * (2.0 / samples)
        if keep_field:
            field_ref[0][p] = g.astype(BF16)
        times = lax.broadcasted_iota(jnp.int32, g.shape, 1)
        muted = jnp.where(times < onset_ref[p], g, 0.0).astype(BF16)
        back = dot(table, muted, NT).astype(BF16)
        for kk in range(own):
            h[kk] = h[kk] + dot(picks[kk], back, TN)
    full = jnp.concatenate(h, axis=1).astype(BF16)
    for j in range(copies):
        h_ref[j] = full


def source_step(v, onset, table, keep_field, copies):
    samples = table.shape[1]
    points, share, _ = onset.shape
    out_shape = [vout((copies,) + v.shape[-2:])]
    if keep_field:
        out_shape.append(jax.ShapeDtypeStruct((points, share, samples), BF16))
    return pl.pallas_call(
        functools.partial(source_kernel, points, keep_field),
        in_specs=[VSPEC] * 3,
        out_specs=[VSPEC] * len(out_shape),
        out_shape=out_shape,
        compiler_params=PARAMS,
        cost_estimate=cost(4 * v.size * samples, 2 * table.size),
        name="source",
    )(vmem(v), vmem(onset), vmem(table))


def adjoint_kernel(k_ref, u_ref, pairs_ref, order_ref, out_ref, o, *rest):
    own, rows, receivers = o.shape
    half = rows // 2
    blocks, _, width = u_ref.shape
    share = width // own
    for kk in range(own):
        parts = [u_ref[j, :, kk * share : (kk + 1) * share] for j in range(blocks)]
        l0 = dot(pairs_ref[...], jnp.concatenate(parts, axis=1), TN).astype(BF16)
        l1 = jnp.concatenate([l0[half:], -l0[:half]], axis=0)
        o[kk] = (dot(l0, k_ref[0, kk]) + dot(l1, k_ref[1, kk])).astype(BF16)
    if not rest:
        flat = o[...].reshape(own * rows, receivers)
        out_ref[...] = dot(order_ref[...], flat, TN).astype(BF16).reshape(out_ref.shape)
        return
    out_buf, sems = rest
    ats = pieces(receivers, 512)
    outs = sends(out_buf, out_ref, sems, ats)
    back = order_ref[...].T
    for i, at in enumerate(ats):
        piece = dot(back, o[:, :, at].reshape(own * rows, at.stop - at.start)).astype(BF16)
        out_buf[:, :, at] = piece.reshape(out_buf.shape[:2] + piece.shape[1:])
        outs[i].start()
    for copy in outs:
        copy.wait()


def adjoint(kernel, u, pairs, order, freq, send):
    _, own, sources, receivers = kernel.shape
    rows = u.shape[1]
    out = (freq, own * rows // freq, receivers)
    sending = [pltpu.VMEM(out, BF16), pltpu.SemaphoreType.DMA((len(pieces(receivers, 512)),))]
    return pl.pallas_call(
        adjoint_kernel,
        in_specs=[VSPEC] * 4,
        out_specs=ANY if send else VSPEC,
        out_shape=jax.ShapeDtypeStruct(out, BF16),
        scratch_shapes=[pltpu.VMEM((own, rows, receivers), BF16)] + (sending if send else []),
        compiler_params=PARAMS,
        cost_estimate=cost(2 * kernel.size * rows, 2 * own * rows * receivers),
        name="adjoint",
    )(vmem(kernel), vmem(u), vmem(pairs), vmem(order))


def after_kernel(x_ref, late_ref, out_ref):
    out_ref[...] = x_ref[...]


def after(x, late):
    return pl.pallas_call(
        after_kernel,
        in_specs=[VSPEC, ANY],
        out_specs=VSPEC,
        out_shape=jax.ShapeDtypeStruct(x.shape, x.dtype),
        compiler_params=PARAMS,
        cost_estimate=cost(x.size, 8 * x.size),
        name="after",
    )(x, late)


def own_rows(q, points, p, scale):
    freq, rows, block = q.shape
    each = rows // points
    mine = q.astype(F32)[:, p * each : (p + 1) * each] * scale
    return mine.reshape(freq * each, block).astype(BF16)


def respectrum_kernel(block, q_ref, first_hbm, onset_ref, table_ref, across_ref, out_hbm, first_ref, out_ref, sem, out_sems):
    copy = pltpu.make_async_copy(first_hbm, first_ref, sem)
    copy.start()
    freq, rows, receivers = q_ref.shape
    samples, _ = across_ref.shape
    points = onset_ref.shape[0]
    ats = pieces(receivers, block)
    outs = sends(out_ref, out_hbm, out_sems, ats)
    for i, at in enumerate(ats):
        wide = at.stop - at.start
        times = lax.broadcasted_iota(jnp.int32, (samples, wide), 0)
        parts = []
        for p in range(points):
            q = dot(across_ref[...], own_rows(q_ref[:, :, at], points, p, 2.0 / samples))
            muted = jnp.where(times < onset_ref[p, :, at], q, 0.0).astype(BF16)
            parts.append(dot(table_ref[...], muted).reshape(freq, rows // points, wide))
        if i == 0:
            copy.wait()
        out_ref[:, :, at] = (first_ref[:, :, at].astype(F32) + jnp.concatenate(parts, axis=1)).astype(BF16)
        outs[i].start()
    for copy in outs:
        copy.wait()


def respectrum(q, first, onset, table, across, block=512):
    freq, rows, receivers = q.shape
    return pl.pallas_call(
        functools.partial(respectrum_kernel, block),
        in_specs=[VSPEC, ANY, VSPEC, VSPEC, VSPEC],
        out_specs=ANY,
        out_shape=jax.ShapeDtypeStruct(q.shape, BF16),
        scratch_shapes=[
            pltpu.VMEM(q.shape, BF16),
            pltpu.VMEM(q.shape, BF16),
            pltpu.SemaphoreType.DMA,
            pltpu.SemaphoreType.DMA((len(pieces(receivers, block)),)),
        ],
        compiler_params=PARAMS,
        cost_estimate=cost(4 * q.size * table.shape[1], 6 * q.size),
        name="respectrum",
    )(vmem(q), hbm(first), vmem(onset), vmem(table), vmem(across))


def update_kernel(q_ref, f_ref, onset_ref, table_ref, out_ref):
    points, block, samples = f_ref.shape
    at = pl.ds(pl.program_id(0) * block, block)
    times = lax.broadcasted_iota(jnp.int32, (block, samples), 1)
    for p in range(points):
        q = dot(own_rows(q_ref[:, :, at], points, p, 2.0 / samples), table_ref[...], TN)
        out_ref[p] = (f_ref[p].astype(F32) + jnp.where(times < onset_ref[p], q, 0.0)).astype(BF16)


def update(q, f, onset, table, block=384):
    points, receivers, samples = f.shape
    trace_block = pl.BlockSpec((points, block, samples), lambda i: (0, i, 0))
    return pl.pallas_call(
        update_kernel,
        grid=(receivers // block,),
        in_specs=[VSPEC, trace_block, pl.BlockSpec((points, block, 1), lambda i: (0, i, 0)), VSPEC],
        out_specs=trace_block,
        out_shape=jax.ShapeDtypeStruct(f.shape, BF16),
        compiler_params=PARAMS,
        cost_estimate=cost(2 * f.size * table.shape[0], 2 * (2 * f.size + q.size)),
        name="update",
    )(vmem(q), f, onset, vmem(table))


def exchange(x, axis):
    return lax.all_to_all(x, axis, split_axis=0, concat_axis=0, tiled=True)


def body(kernel, focusing_in, onset_src, onset_rec):
    freq = lax.axis_size("freq")
    rec = lax.axis_size("rec")
    _, own, sources, receivers = kernel.shape
    points, _, samples = focusing_in.shape
    share = sources // rec
    lines, width = freq * points * 2, own * share
    table = make_table(freq, own, samples)
    order = make_order(freq, points, own)
    pairs = make_pairs(freq, points)
    start = spec = spectrum(focusing_in, table, freq)
    own_sources = lax.dynamic_slice_in_dim(after(onset_src, start), lax.axis_index("rec") * share, share, 1)
    late = src_onsets = own_sources[:, :, None]
    for step in range(ITERS):
        last = step == ITERS - 1
        part, held = product(kernel, exchange(spec, "freq"), order, pairs, late, rec)
        v = exchange(part.reshape(rec * freq, points * 2, width), ("rec", "freq")).reshape(rec, lines, width)
        h, *field = source_step(v, src_onsets, table, last, rec)
        u = exchange(h.reshape(rec * freq, points * 2, width), ("rec", "freq")).reshape(rec, lines, width)
        q = adjoint(held, u, pairs, order, freq, not last)
        if last:
            return update(exchange(q, "freq"), focusing_in, late, table), field[0]
        row, across = after(onset_rec, q)[:, None, :], lax.optimization_barrier(table).T
        spec = respectrum(exchange(q, "freq"), start, row, table, across)
        late = after(onset_rec, spec)[:, :, None]


def solution(mesh):
    placed = (
        P(None, "freq", None, "rec"),
        P("freq", "rec", None),
        P("freq", None),
        P("freq", "rec"),
    )
    return jax.shard_map(
        body,
        mesh=mesh,
        in_specs=placed,
        out_specs=(P("freq", "rec", None), P("freq", "rec", None)),
        check_vma=False,
    )
```

```python
import functools

import jax
import jax.numpy as jnp
import numpy as np
from jax import lax
from jax.experimental import pallas as pl
from jax.experimental.pallas import tpu as pltpu
from jax.sharding import PartitionSpec as P

LOW = 8
ITERS = 2
F32 = jnp.float32
BF16 = jnp.bfloat16
NN = (((1,), (0,)), ((), ()))
NT = (((1,), (1,)), ((), ()))
TN = (((0,), (0,)), ((), ()))


def dot(a, b, dims=NN):
    return lax.dot_general(a, b, dims, preferred_element_type=F32)


def make_table(freq, own, samples):
    k = np.arange(freq * own)[:, None] + LOW
    t = np.arange(samples)[None, :]
    phase = ((k * t) % samples).astype(np.float32) * np.float32(2.0 * 3.141592653589793 / samples)
    both = np.stack([np.cos(phase), -np.sin(phase)]).astype(np.float32)
    rows = both.reshape(2, freq, own, samples).transpose(1, 0, 2, 3)
    return jnp.asarray(rows.reshape(freq * 2 * own, samples), BF16)


def make_order(freq, points, own):
    n = freq * points * 2 * own
    rows = np.arange(n).reshape(freq, points, 2, own).transpose(3, 2, 0, 1).reshape(n)
    return jnp.asarray(np.eye(n, dtype=np.float32)[rows], BF16)


def make_pairs(freq, points):
    n = freq * points * 2
    rows = np.arange(n).reshape(2, freq, points).transpose(1, 2, 0).reshape(n)
    return jnp.asarray(np.eye(n, dtype=np.float32)[rows], BF16)


VSPEC = pl.BlockSpec(memory_space=pltpu.VMEM)
ANY = pl.BlockSpec(memory_space=pl.ANY)
PARAMS = pltpu.CompilerParams(vmem_limit_bytes=24 << 20)


def vmem(x):
    return pltpu.with_memory_space_constraint(x, pltpu.VMEM)


def hbm(x):
    return pltpu.with_memory_space_constraint(x, pltpu.HBM)


def vout(shape):
    return pltpu.VMEM(shape, BF16)


def cost(flops, bytes_accessed):
    return pl.CostEstimate(flops=int(flops), transcendentals=0, bytes_accessed=int(bytes_accessed))


def pieces(length, size, first=0):
    edges = [0] + list(range(first or size, length, size)) + [length]
    return [slice(a, b) for a, b in zip(edges[:-1], edges[1:])]


def sends(buf, out, sems, ats):
    return [pltpu.make_async_copy(buf.at[:, :, at], out.at[:, :, at], sems.at[i]) for i, at in enumerate(ats)]


def spectrum_kernel(f_hbm, table_hbm, out_hbm, f_buf, table_buf, out_ref, sems, out_sems):
    freq = out_ref.shape[0]
    points, receivers, _ = f_buf.shape
    ats = pieces(receivers, 512, 256)
    outs = sends(out_ref, out_hbm, out_sems, ats)
    copies = [pltpu.make_async_copy(f_hbm.at[:, at], f_buf.at[:, at], sems.at[i]) for i, at in enumerate(ats)]
    table_copy = pltpu.make_async_copy(table_hbm, table_buf, sems.at[len(ats)])
    table_copy.start()
    copies[0].start()
    table_copy.wait()
    copies[1].start()
    for i, at in enumerate(ats):
        copies[i].wait()
        if i + 2 < len(ats):
            copies[i + 2].start()
        parts = [dot(table_buf[...], f_buf[p, at], NT) for p in range(points)]
        parts = [s.reshape(freq, s.shape[0] // freq, s.shape[1]) for s in parts]
        out_ref[:, :, at] = jnp.concatenate(parts, axis=1).astype(BF16)
        outs[i].start()
    for copy in outs:
        copy.wait()


def spectrum(f, table, freq):
    points, receivers, _ = f.shape
    rows = points * table.shape[0] // freq
    return pl.pallas_call(
        spectrum_kernel,
        in_specs=[ANY, ANY],
        out_specs=ANY,
        out_shape=jax.ShapeDtypeStruct((freq, rows, receivers), BF16),
        scratch_shapes=[
            pltpu.VMEM(f.shape, BF16),
            pltpu.VMEM(table.shape, BF16),
            pltpu.VMEM((freq, rows, receivers), BF16),
            pltpu.SemaphoreType.DMA((len(pieces(receivers, 512, 256)) + 1,)),
            pltpu.SemaphoreType.DMA((len(pieces(receivers, 512, 256)),)),
        ],
        compiler_params=PARAMS,
        cost_estimate=cost(2 * f.size * table.shape[0], 2 * (f.size + freq * rows * receivers)),
        name="spectrum",
    )(hbm(f), hbm(table))


def product_kernel(k_hbm, x_ref, order_ref, pairs_ref, late_ref, out_ref, k_buf, w, sems):
    own, rows, receivers = w.shape
    half = rows // 2
    blocks, _, width = out_ref.shape
    share = width // own
    copies = [pltpu.make_async_copy(k_hbm.at[:, kk], k_buf.at[:, kk], sems.at[kk]) for kk in range(own)]
    for copy in copies[:2]:
        copy.start()
    x = x_ref[...].reshape(own * rows, receivers)
    w[...] = dot(order_ref[...], x).astype(BF16).reshape(w.shape)
    g = []
    for kk in range(own):
        w0 = w[kk]
        w1 = jnp.concatenate([-w0[half:], w0[:half]], axis=0)
        copies[kk].wait()
        if kk + 2 < own:
            copies[kk + 2].start()
        total = dot(k_buf[0, kk], w0, NT) + dot(k_buf[1, kk], w1, NT)
        g.append(dot(pairs_ref[...], total.astype(BF16), NT))
    for j in range(blocks):
        parts = [g[kk][:, j * share : (j + 1) * share] for kk in range(own)]
        out_ref[j] = jnp.concatenate(parts, axis=1).astype(BF16)


def product(kernel, x, order, pairs, late, blocks):
    _, own, sources, receivers = kernel.shape
    rows = order.shape[0] // own
    width = own * sources // blocks
    return pl.pallas_call(
        product_kernel,
        in_specs=[ANY, VSPEC, VSPEC, VSPEC, ANY],
        out_specs=[VSPEC, VSPEC],
        out_shape=[vout((blocks, rows, width)), vout(kernel.shape)],
        scratch_shapes=[pltpu.VMEM((own, rows, receivers), BF16), pltpu.SemaphoreType.DMA((own,))],
        compiler_params=PARAMS,
        cost_estimate=cost(2 * kernel.size * rows, 2 * (kernel.size + x.size)),
        name="product",
    )(hbm(kernel), vmem(x), vmem(order), vmem(pairs), late)


def source_kernel(points, keep_field, v_ref, onset_ref, table_ref, h_ref, *field_ref):
    rows, samples = table_ref.shape
    copies, lines, width = h_ref.shape
    share = onset_ref.shape[1]
    own = width // share
    table = table_ref[...]
    v = v_ref[...].astype(F32)
    if v.ndim == 3:
        v = jnp.sum(v, axis=0)
    v = v.astype(BF16)
    row = lax.broadcasted_iota(jnp.int32, (rows, lines), 0)
    line = lax.broadcasted_iota(jnp.int32, (rows, lines), 1)
    device, part, mine = row // (2 * own), row // own % 2, row % own
    h = [jnp.zeros((lines, share), F32) for _ in range(own)]
    for p in range(points):
        at = (device * points + p) * 2 + part
        picks = [jnp.where((line == at) & (mine == kk), 1.0, 0.0).astype(BF16) for kk in range(own)]
        full = jnp.zeros((rows, share), F32)
        for kk in range(own):
            full = full + dot(picks[kk], v[:, kk * share : (kk + 1) * share])
        g = dot(full.astype(BF16), table, TN) * (2.0 / samples)
        if keep_field:
            field_ref[0][p] = g.astype(BF16)
        times = lax.broadcasted_iota(jnp.int32, g.shape, 1)
        muted = jnp.where(times < onset_ref[p], g, 0.0).astype(BF16)
        back = dot(table, muted, NT).astype(BF16)
        for kk in range(own):
            h[kk] = h[kk] + dot(picks[kk], back, TN)
    full = jnp.concatenate(h, axis=1).astype(BF16)
    for j in range(copies):
        h_ref[j] = full


def source_step(v, onset, table, keep_field, copies):
    samples = table.shape[1]
    points, share, _ = onset.shape
    out_shape = [vout((copies,) + v.shape[-2:])]
    if keep_field:
        out_shape.append(jax.ShapeDtypeStruct((points, share, samples), BF16))
    return pl.pallas_call(
        functools.partial(source_kernel, points, keep_field),
        in_specs=[VSPEC] * 3,
        out_specs=[VSPEC] * len(out_shape),
        out_shape=out_shape,
        compiler_params=PARAMS,
        cost_estimate=cost(4 * v.size * samples, 2 * table.size),
        name="source",
    )(vmem(v), vmem(onset), vmem(table))


def adjoint_kernel(k_ref, u_ref, pairs_ref, order_ref, out_ref, o, *rest):
    own, rows, receivers = o.shape
    half = rows // 2
    blocks, _, width = u_ref.shape
    share = width // own
    for kk in range(own):
        parts = [u_ref[j, :, kk * share : (kk + 1) * share] for j in range(blocks)]
        l0 = dot(pairs_ref[...], jnp.concatenate(parts, axis=1), TN).astype(BF16)
        l1 = jnp.concatenate([l0[half:], -l0[:half]], axis=0)
        o[kk] = (dot(l0, k_ref[0, kk]) + dot(l1, k_ref[1, kk])).astype(BF16)
    if not rest:
        flat = o[...].reshape(own * rows, receivers)
        out_ref[...] = dot(order_ref[...], flat, TN).astype(BF16).reshape(out_ref.shape)
        return
    out_buf, sems = rest
    ats = pieces(receivers, 512)
    outs = sends(out_buf, out_ref, sems, ats)
    back = order_ref[...].T
    for i, at in enumerate(ats):
        piece = dot(back, o[:, :, at].reshape(own * rows, at.stop - at.start)).astype(BF16)
        out_buf[:, :, at] = piece.reshape(out_buf.shape[:2] + piece.shape[1:])
        outs[i].start()
    for copy in outs:
        copy.wait()


def adjoint(kernel, u, pairs, order, freq, send):
    _, own, sources, receivers = kernel.shape
    rows = u.shape[1]
    out = (freq, own * rows // freq, receivers)
    sending = [pltpu.VMEM(out, BF16), pltpu.SemaphoreType.DMA((len(pieces(receivers, 512)),))]
    return pl.pallas_call(
        adjoint_kernel,
        in_specs=[VSPEC] * 4,
        out_specs=ANY if send else VSPEC,
        out_shape=jax.ShapeDtypeStruct(out, BF16),
        scratch_shapes=[pltpu.VMEM((own, rows, receivers), BF16)] + (sending if send else []),
        compiler_params=PARAMS,
        cost_estimate=cost(2 * kernel.size * rows, 2 * own * rows * receivers),
        name="adjoint",
    )(vmem(kernel), vmem(u), vmem(pairs), vmem(order))


def after_kernel(x_ref, late_ref, out_ref):
    out_ref[...] = x_ref[...]


def after(x, late):
    return pl.pallas_call(
        after_kernel,
        in_specs=[VSPEC, ANY],
        out_specs=VSPEC,
        out_shape=jax.ShapeDtypeStruct(x.shape, x.dtype),
        compiler_params=PARAMS,
        cost_estimate=cost(x.size, 8 * x.size),
        name="after",
    )(x, late)


def own_rows(q, points, p, scale):
    freq, rows, block = q.shape
    each = rows // points
    mine = q.astype(F32)[:, p * each : (p + 1) * each] * scale
    return mine.reshape(freq * each, block).astype(BF16)


def respectrum_kernel(block, q_ref, first_hbm, onset_ref, table_ref, across_ref, out_hbm, first_ref, out_ref, sem, out_sems):
    copy = pltpu.make_async_copy(first_hbm, first_ref, sem)
    copy.start()
    freq, rows, receivers = q_ref.shape
    samples, _ = across_ref.shape
    points = onset_ref.shape[0]
    ats = pieces(receivers, block)
    outs = sends(out_ref, out_hbm, out_sems, ats)
    for i, at in enumerate(ats):
        wide = at.stop - at.start
        times = lax.broadcasted_iota(jnp.int32, (samples, wide), 0)
        parts = []
        for p in range(points):
            q = dot(across_ref[...], own_rows(q_ref[:, :, at], points, p, 2.0 / samples))
            muted = jnp.where(times < onset_ref[p, :, at], q, 0.0).astype(BF16)
            parts.append(dot(table_ref[...], muted).reshape(freq, rows // points, wide))
        if i == 0:
            copy.wait()
        out_ref[:, :, at] = (first_ref[:, :, at].astype(F32) + jnp.concatenate(parts, axis=1)).astype(BF16)
        outs[i].start()
    for copy in outs:
        copy.wait()


def respectrum(q, first, onset, table, across, block=512):
    freq, rows, receivers = q.shape
    return pl.pallas_call(
        functools.partial(respectrum_kernel, block),
        in_specs=[VSPEC, ANY, VSPEC, VSPEC, VSPEC],
        out_specs=ANY,
        out_shape=jax.ShapeDtypeStruct(q.shape, BF16),
        scratch_shapes=[
            pltpu.VMEM(q.shape, BF16),
            pltpu.VMEM(q.shape, BF16),
            pltpu.SemaphoreType.DMA,
            pltpu.SemaphoreType.DMA((len(pieces(receivers, block)),)),
        ],
        compiler_params=PARAMS,
        cost_estimate=cost(4 * q.size * table.shape[1], 6 * q.size),
        name="respectrum",
    )(vmem(q), hbm(first), vmem(onset), vmem(table), vmem(across))


def update_kernel(q_ref, f_ref, onset_ref, table_ref, out_ref):
    points, block, samples = f_ref.shape
    at = pl.ds(pl.program_id(0) * block, block)
    lanes = 128
    times = lax.broadcasted_iota(jnp.int32, (block, samples), 1)
    for p in range(points):
        column = jnp.broadcast_to(onset_ref[p, :, at], (lanes, block)).T
        onset = jnp.concatenate([column] * (samples // lanes), axis=1)
        q = dot(own_rows(q_ref[:, :, at], points, p, 2.0 / samples), table_ref[...], TN)
        out_ref[p] = (f_ref[p].astype(F32) + jnp.where(times < onset, q, 0.0)).astype(BF16)


def update(q, f, onset, table, block=384):
    points, receivers, samples = f.shape
    trace_block = pl.BlockSpec((points, block, samples), lambda i: (0, i, 0))
    return pl.pallas_call(
        update_kernel,
        grid=(receivers // block,),
        in_specs=[VSPEC, trace_block, VSPEC, VSPEC],
        out_specs=trace_block,
        out_shape=jax.ShapeDtypeStruct(f.shape, BF16),
        compiler_params=PARAMS,
        cost_estimate=cost(2 * f.size * table.shape[0], 2 * (2 * f.size + q.size)),
        name="update",
    )(vmem(q), f, vmem(onset), vmem(table))


def exchange(x, axis):
    return lax.all_to_all(x, axis, split_axis=0, concat_axis=0, tiled=True)


def body(kernel, focusing_in, onset_src, onset_rec):
    freq = lax.axis_size("freq")
    rec = lax.axis_size("rec")
    _, own, sources, receivers = kernel.shape
    points, _, samples = focusing_in.shape
    share = sources // rec
    lines, width = freq * points * 2, own * share
    table = make_table(freq, own, samples)
    order = make_order(freq, points, own)
    pairs = make_pairs(freq, points)
    start = spec = spectrum(focusing_in, table, freq)
    own_sources = lax.dynamic_slice_in_dim(after(onset_src, start), lax.axis_index("rec") * share, share, 1)
    late = src_onsets = own_sources[:, :, None]
    for step in range(ITERS):
        last = step == ITERS - 1
        part, held = product(kernel, exchange(spec, "freq"), order, pairs, late, rec)
        v = exchange(part.reshape(rec * freq, points * 2, width), ("rec", "freq")).reshape(rec, lines, width)
        h, *field = source_step(v, src_onsets, table, last, rec)
        u = exchange(h.reshape(rec * freq, points * 2, width), ("rec", "freq")).reshape(rec, lines, width)
        q = adjoint(held, u, pairs, order, freq, not last)
        if last:
            return update(exchange(q, "freq"), focusing_in, row, table), field[0]
        row, across = after(onset_rec, q)[:, None, :], lax.optimization_barrier(table).T
        spec = respectrum(exchange(q, "freq"), start, row, table, across)


def solution(mesh):
    placed = (
        P(None, "freq", None, "rec"),
        P("freq", "rec", None),
        P("freq", None),
        P("freq", "rec"),
    )
    return jax.shard_map(
        body,
        mesh=mesh,
        in_specs=placed,
        out_specs=(P("freq", "rec", None), P("freq", "rec", None)),
        check_vma=False,
    )
```
